256 devices in a mesh: src: 32 (over y, z), tm: 8 (over x, core).
Axes of the slice: x: 4, y: 4, z: 8, core: 2. Of those that a mesh axis runs over, the one named last changes fastest.
Arguments:
- green: bfloat16 [8, 4096, 128, 128], P('tm', 'src'), may hold values from -0.046875 to 0.046875
- block_rows: int32 [8, 4096], P('tm', 'src'), may hold values from 0 to 31
- block_cols: int32 [8, 4096], P('tm', 'src'), may hold values from 0 to 31
- block_live: int32 [8, 4096], P('tm', 'src'), may hold values from 0 to 1, as said below
- data: float32 [8, 4096, 128], P('tm', 'src'), may hold values from -6 to 6
- row_weight: float32 [8, 4096], P('tm', 'src'), may hold values from 0.3 to 9
- source_gain: float32 [131072], P('src'), may hold values from 0.2 to 3
Outputs:
- solution: float32 [131072, 128], P(('src', 'tm'))
- residual: float32 [8, 4096, 128], P('tm', 'src')
- misfit: float32 [2, 128], replicated
The draws below stay inside these ranges and needn't reach their ends.
Inputs may be any that keep to these rules, and one draw needn't show every extreme that they name: `block_live`: within one device's 128 slots every slot is live with the same chance, a chance that differs from device to device; in some device all 128 slots are live.
All inputs are finite; a program needn't handle non-finite values.
Results may differ from the reference program's by a relative error of at most 0.0038.
Values may be sent and summed in bfloat16 or wider, within the bound.
A program may use at most 128 MiB of HBM per device.

```python
import math
import jax
import jax.numpy as jnp
from jax import lax

BS = 128
DATASETS = 128
NB = 128
ROWB_DEV = 1
ITERS = 2
WINDOWS = 8
GROUPS = 32
RB = 32
CB = 32
WROWS = 4096
ROWS = 32768
SOURCES = 131072


def draw_block_live(key, part):
    first_key, second_key, third_key = jax.random.split(key, 3)
    devices = WINDOWS * GROUPS
    levels = jax.random.randint(first_key, (devices,), 2, 9)
    chosen = jax.random.randint(second_key, (), 0, devices)
    levels = jnp.where(jnp.arange(devices, dtype=jnp.int32) == chosen, 8, levels)
    coin_flips = jax.random.randint(third_key, (devices, NB), 0, 8)
    live_slots = (coin_flips < levels[:, None]).astype(jnp.int32)
    return live_slots.reshape(WINDOWS, GROUPS * NB)


def draw_row_weight(key, part):
    count_all = WINDOWS * WROWS
    position = jnp.arange(count_all, dtype=jnp.float32) / (count_all - 1)
    rising = 1.0 + 2.0 * position
    spread = jnp.exp(jax.random.uniform(key, (count_all,), jnp.float32, math.log(0.3), math.log(3.0)))
    return (rising * spread).reshape(WINDOWS, WROWS)


def draw_source_gain(key, part):
    position = jnp.arange(SOURCES, dtype=jnp.float32) / (SOURCES - 1)
    rising = 1.0 + 2.0 * position
    spread = jnp.exp(jax.random.uniform(key, (SOURCES,), jnp.float32, math.log(0.2), 0.0))
    return rising * spread


def place_ends(array, rng, smallest, high):
    place = [jax.random.randint(jax.random.fold_in(rng, axis), (), 0, length) for axis, length in enumerate(array.shape)]
    longest = array.shape.index(max(array.shape))
    neighbour = place[:longest] + [(place[longest] + 1) % array.shape[longest]] + place[longest + 1:]
    return array.at[tuple(place)].set(smallest).at[tuple(neighbour)].set(high)


def level_of(own_key, shape, shards, smallest, largest):
    level = 1.0
    for dim, parts in shards:
        heights = jax.random.uniform(jax.random.fold_in(jax.random.fold_in(own_key, 6), dim), (parts,), jnp.float32, smallest / len(shards), largest / len(shards))
        level = level * jnp.repeat(jnp.exp(heights), shape[dim] // parts).reshape((-1,) + (1,) * (len(shape) - 1 - dim))
    return level


def gaussian(rng, shape, scale, most, pieces=(), kind=jnp.bfloat16):
    drawn = jax.random.normal(rng, shape, jnp.float32) * scale
    if len(pieces) > 0:
        drawn = level_of(rng, shape, pieces, -0.22, 0.18) * drawn
    return jnp.clip(drawn, min=-most, max=most).astype(kind)


def setup_inputs(seed: int = 0) -> dict:
    seeds = jax.random.split(jax.random.key(seed), 8)
    green = gaussian(seeds[0], (WINDOWS, GROUPS * NB, BS, BS), (BS * NB // ROWB_DEV) ** -0.5, 0.046875, ((0, 8), (1, 32)))
    block_rows = place_ends(jax.random.randint(seeds[1], (WINDOWS, GROUPS * NB), 0, RB), jax.random.fold_in(seeds[1], 1), 0, RB - 1).astype(jnp.int32)
    block_cols = place_ends(jax.random.randint(seeds[2], (WINDOWS, GROUPS * NB), 0, CB), jax.random.fold_in(seeds[2], 1), 0, CB - 1).astype(jnp.int32)
    block_live = draw_block_live(jax.random.fold_in(seeds[7], 71), 0)
    data = gaussian(seeds[4], (WINDOWS, WROWS, DATASETS), 1.0, 6.0, ((0, 8), (1, 32)), jnp.float32)
    row_weight = draw_row_weight(jax.random.fold_in(seeds[7], 71), 0)
    source_gain = draw_source_gain(jax.random.fold_in(seeds[7], 71), 0)
    return {"green": green, "block_rows": block_rows, "block_cols": block_cols, "block_live": block_live, "data": data, "row_weight": row_weight, "source_gain": source_gain}


HIGH = lax.Precision.HIGHEST
EPSILON = 1e-6


def forward_product(blocks_all, rows_all, cols_all, live_all, scaled):
    grouped = scaled.reshape(GROUPS, CB, BS, DATASETS)

    def one_window(window):
        def advance(summed, group):
            blocks = blocks_all[window, group].astype(jnp.float32)
            picked = grouped[group][cols_all[window, group]].astype(jnp.float32)
            products = jnp.einsum("kac,kcr->kar", blocks, picked, precision=HIGH)
            products = products * live_all[window, group].astype(jnp.float32)[:, None, None]
            return summed.at[rows_all[window, group]].add(products), None

        start_sum = jnp.zeros((RB, BS, DATASETS), jnp.float32)
        summed, ignored = lax.scan(advance, start_sum, jnp.arange(GROUPS, dtype=jnp.int32))
        return summed

    image = lax.map(one_window, jnp.arange(WINDOWS, dtype=jnp.int32))
    return image.reshape(WINDOWS, WROWS, DATASETS)


def adjoint_product(blocks_all, rows_all, cols_all, live_all, sent):
    row_groups = sent.reshape(WINDOWS, RB, BS, DATASETS)

    def one_group(group):
        def advance(summed, window):
            blocks = blocks_all[window, group].astype(jnp.float32)
            picked = row_groups[window][rows_all[window, group]].astype(jnp.float32)
            products = jnp.einsum("kac,kar->kcr", blocks, picked, precision=HIGH)
            products = products * live_all[window, group].astype(jnp.float32)[:, None, None]
            return summed.at[cols_all[window, group]].add(products), None

        start_sum = jnp.zeros((CB, BS, DATASETS), jnp.float32)
        summed, ignored = lax.scan(advance, start_sum, jnp.arange(WINDOWS, dtype=jnp.int32))
        return summed

    grads = lax.map(one_group, jnp.arange(GROUPS, dtype=jnp.int32))
    return grads.reshape(SOURCES, DATASETS)


def reference(green, block_rows, block_cols, block_live, data, row_weight, source_gain):
    blocks_all = green.reshape(WINDOWS, GROUPS, NB, BS, BS)
    rows_all = block_rows.reshape(WINDOWS, GROUPS, NB)
    cols_all = block_cols.reshape(WINDOWS, GROUPS, NB)
    live_all = block_live.reshape(WINDOWS, GROUPS, NB)
    weight = row_weight[:, :, None]
    gain = source_gain[:, None]
    residual = weight * data
    sent = (weight * residual).astype(jnp.bfloat16)
    steepest = gain * adjoint_product(blocks_all, rows_all, cols_all, live_all, sent)
    gamma_now = jnp.sum(steepest * steepest, axis=0)
    direction = steepest
    solution = jnp.zeros((SOURCES, DATASETS), jnp.float32)
    misfits = []
    for iteration in range(ITERS):
        scaled = (gain * direction).astype(jnp.bfloat16)
        image = weight * forward_product(blocks_all, rows_all, cols_all, live_all, scaled)
        image_norm = jnp.sum(image * image, axis=(0, 1))
        step_size = gamma_now / (image_norm + EPSILON)
        solution = solution + step_size * direction
        residual = residual - step_size * image
        misfits.append(jnp.sum(residual * residual, axis=(0, 1)) / ROWS)
        if iteration + 1 < ITERS:
            sent = (weight * residual).astype(jnp.bfloat16)
            steepest = gain * adjoint_product(blocks_all, rows_all, cols_all, live_all, sent)
            gamma_next = jnp.sum(steepest * steepest, axis=0)
            direction = steepest + (gamma_next / (gamma_now + EPSILON)) * direction
            gamma_now = gamma_next
    return solution, residual, jnp.stack(misfits)
```

```python
import functools

import jax
import jax.numpy as jnp
from jax import lax
from jax.experimental import pallas as pl
from jax.experimental.pallas import tpu as pltpu
from jax.sharding import PartitionSpec as P

MESH = pl.DeviceIdType.MESH
EPSILON = 1e-06
NZ = 8
NC = 2
BS = 128
F32 = jnp.float32
BF16 = jnp.bfloat16


STEPS = 32000.0


def outward(n):
    return sorted(range(1, n), key=lambda d: -min(d, n - d))


def pack(ref, v):
    top = jnp.maximum(jnp.max(jnp.abs(v), axis=0, keepdims=True), 1e-30)
    e = jnp.ceil(jnp.log2(top))
    q = jnp.floor(v * (jnp.exp2(-e) * STEPS) + 0.5)
    ref[0:BS, :] = q.astype(jnp.int32).astype(jnp.int16)
    ref[BS : BS + 16, :] = jnp.broadcast_to(e.astype(jnp.int32), (16, BS)).astype(jnp.int16)


def unpack(ref):
    e = ref[BS : BS + 16, :].astype(jnp.int32).astype(F32)[0:1]
    return ref[0:BS, :].astype(jnp.int32).astype(F32) * (jnp.exp2(e) * (1.0 / STEPS))


def kernel(
    ny, nx, total_rows, slots, cb,
    tab, green_hbm, data, weight, gain,
    sol_out, res_out, mis_out,
    green, ag, sums, core_send, core_recv, x_send, x_recv, tb, y_send, y_recv, z_send, z_recv,
    wcol, gcol, steep, own, ar_z, ar_p, ar_c,
    ssem, rsem, lsem,
):
    nz, nc = NZ, NC
    rb = ny * nz
    per = cb // (nx * nc)
    s = lax.axis_index("src")
    t = lax.axis_index("tm")
    y, z = s // nz, s % nz
    x, c = t // nc, t % nc

    def zdev(d):
        return (y * nz + (z + d) % nz, t)

    def ydev(d):
        return (((y + d) % ny) * nz + z, t)

    def xdev(d):
        return (s, ((x + d) % nx) * nc + c)

    def cdev():
        return (s, x * nc + (1 - c))

    counter = [0]

    def rcopy(src, dst, dev):
        i = counter[0]
        counter[0] += 1
        return pltpu.make_async_remote_copy(
            src_ref=src, dst_ref=dst, send_sem=ssem.at[i], recv_sem=rsem.at[i],
            device_id=dev, device_id_type=MESH,
        )

    load = pltpu.make_async_copy(green_hbm, green, lsem)
    load.start()

    def pdev(d):
        return (((y + d // nx) % ny) * nz + z, ((x + d % nx) % nx) * nc + c)

    peers = [zdev(d) for d in range(1, nz)] + [pdev(d) for d in range(1, ny * nx)] + [cdev()]
    barrier = pltpu.get_barrier_semaphore()
    for dev in peers:
        pl.semaphore_signal(barrier, inc=1, device_id=dev, device_id_type=MESH)

    wcol[...] = jnp.transpose(jnp.broadcast_to(weight[...], (BS, BS)))
    for i in range(per):
        row = gain[pl.ds(t * per + i, 1), :]
        gcol[i] = jnp.transpose(jnp.broadcast_to(row, (BS, BS)))
    sums[slots] = jnp.zeros((BS, BS), F32)
    res_out[...] = wcol[...] * data[...]
    pl.semaphore_wait(barrier, len(peers))

    def gather_src(it):
        ag[it, y, z] = jnp.transpose(wcol[...] * res_out[...]).astype(BF16)
        mine = ag.at[it, y, z]
        zc = {d: rcopy(mine, mine, zdev(d)) for d in outward(nz)}
        yc = [rcopy(mine, mine, ydev(e)) for e in outward(ny)]
        for d in outward(nz):
            zc[d].start()
        for cp in yc:
            cp.start()
        for d in reversed(outward(nz)):
            zc[d].wait_recv()
            got = ag.at[it, y, (z + nz - d) % nz]
            for e in outward(ny):
                cp = rcopy(got, got, ydev(e))
                cp.start()
                yc.append(cp)
        for cp in yc:
            cp.wait()
        for d in zc:
            zc[d].wait_send()

    def adjoint(it):
        def slot(k, carry):
            r = tab[0, k]
            p = jnp.dot(ag[it, r // nz, r % nz], green[k], preferred_element_type=F32)
            sums[k] = p + sums[tab[2, k]]
            return carry

        lax.fori_loop(0, slots, slot, 0, unroll=4)

    def forward(it):
        def slot(k, carry):
            p = jnp.dot(green[k], tb[it, tab[1, k]], preferred_element_type=F32)
            sums[k] = p + sums[tab[3, k]]
            return carry

        lax.fori_loop(0, slots, slot, 0, unroll=4)

    def scatter_tm(it):
        order = outward(nx) + [0]
        cc = []
        for d in order:
            xx = (x + d) % nx
            for i in range(per):
                b = xx * nc * per + (1 - c) * per + i
                core_send[it, xx * per + i] = sums[tab[4, b]]
            part = pl.ds(xx * per, per)
            cp = rcopy(core_send.at[it, part], core_recv.at[it, part], cdev())
            cp.start()
            cc.append(cp)
        xc = []
        for j, d in enumerate(order):
            xx = (x + d) % nx
            cc[j].wait()
            for i in range(per):
                b = xx * nc * per + c * per + i
                v = sums[tab[4, b]] + core_recv[it, xx * per + i]
                if d:
                    pack(x_send.at[it, d - 1, i], v)
                else:
                    own[i] = v
            if d:
                cp = rcopy(x_send.at[it, d - 1], x_recv.at[it, d - 1], xdev(d))
                cp.start()
                xc.append(cp)
        for cp in xc:
            cp.wait()
        gamma = jnp.zeros((1, BS), F32)
        for i in range(per):
            v = own[i]
            for d in range(1, nx):
                v = v + unpack(x_recv.at[it, d - 1, i])
            st = gcol[i] * jnp.transpose(v)
            steep[it, i] = st
            gamma = gamma + jnp.sum(st * st, axis=0, keepdims=True)
            tb[it, t * per + i] = (gcol[i] * st).astype(BF16)
        return gamma

    def gather_tm(it):
        def part(xx, cc):
            return tb.at[it, pl.ds((xx * nc + cc) * per, per)]

        mine = part(x, c)
        xc = {d: rcopy(mine, mine, xdev(d)) for d in outward(nx)}
        for d in xc:
            xc[d].start()
        fc = [rcopy(mine, mine, cdev())]
        fc[0].start()
        for d in reversed(outward(nx)):
            xc[d].wait_recv()
            got = part((x + nx - d) % nx, c)
            cp = rcopy(got, got, cdev())
            cp.start()
            fc.append(cp)
        for cp in fc:
            cp.wait()
        for d in xc:
            xc[d].wait_send()

    def scatter_src(it):
        order = outward(nz) + [0]
        yc = {}
        for d in order:
            zz = (z + d) % nz
            for e in outward(ny):
                pack(y_send.at[it, e - 1, zz], sums[tab[5, ((y + e) % ny) * nz + zz]])
                yc[d, e] = rcopy(y_send.at[it, e - 1, zz], y_recv.at[it, e - 1, zz], ydev(e))
                yc[d, e].start()
        zc = []
        for d in order:
            zz = (z + d) % nz
            v = sums[tab[5, y * nz + zz]]
            for e in range(1, ny):
                yc[d, e].wait()
                v = v + unpack(y_recv.at[it, e - 1, zz])
            if d:
                pack(z_send.at[it, d - 1], v)
                cp = rcopy(z_send.at[it, d - 1], z_recv.at[it, d - 1], zdev(d))
                cp.start()
                zc.append(cp)
        for cp in zc:
            cp.wait()
        for d in range(1, nz):
            v = v + unpack(z_recv.at[it, d - 1])
        return wcol[...] * v

    def all_reduce(n, v):
        for ref, me, count, dev in (
            (ar_z, z, nz, zdev), (ar_p, y * nx + x, ny * nx, pdev), (ar_c, c, nc, None),
        ):
            ref[n, me] = v
            copies = [
                rcopy(ref.at[n, me], ref.at[n, me], dev(d) if dev else cdev())
                for d in range(count - 1, 0, -1)
            ]
            for cp in copies:
                cp.start()
            for cp in copies:
                cp.wait()
            v = ref[n, 0]
            for j in range(1, count):
                v = v + ref[n, j]
        return v

    def rowsum(a):
        return jnp.sum(a, axis=0, keepdims=True)

    gather_src(0)
    load.wait()
    adjoint(0)
    gamma0 = scatter_tm(0)
    gather_tm(0)
    forward(0)
    image0 = scatter_src(0)
    norms = jnp.concatenate([gamma0, rowsum(image0 * image0), jnp.zeros((6, BS), F32)], axis=0)
    norms = all_reduce(0, norms)
    gamma0 = norms[0:1]
    norm0 = norms[1:2]
    alpha0 = gamma0 / (norm0 + EPSILON)
    own[per] = image0
    residual = res_out[...] - alpha0 * image0
    res_out[...] = residual
    gather_src(1)
    adjoint(1)
    gamma1 = scatter_tm(1)
    gather_tm(1)
    forward(1)
    part1 = scatter_src(1)
    image0 = own[per]
    residual = res_out[...]
    norms = jnp.concatenate(
        [
            gamma1, rowsum(part1 * part1), rowsum(part1 * image0), rowsum(residual * residual),
            rowsum(residual * part1), rowsum(residual * image0), jnp.zeros((2, BS), F32),
        ],
        axis=0,
    )
    norms = all_reduce(1, norms)
    gamma1 = norms[0:1]
    beta = gamma1 / (gamma0 + EPSILON)
    norm1 = norms[1:2] + beta * (2.0 * norms[2:3] + beta * norm0)
    alpha1 = gamma1 / (norm1 + EPSILON)
    cross = norms[4:5] + beta * norms[5:6]
    misfit1 = norms[3:4] + alpha1 * (alpha1 * norm1 - 2.0 * cross)
    mis_out[0:1, :] = norms[3:4] / total_rows
    mis_out[1:2, :] = misfit1 / total_rows
    res_out[...] = residual - alpha1 * (part1 + beta * image0)
    for i in range(per):
        sol_out[pl.ds(i * BS, BS), :] = (alpha0 + alpha1 * beta) * steep[0, i] + alpha1 * steep[1, i]


def tables(rows, cols, live, slots, rb, cb):
    j = jnp.arange(slots, dtype=jnp.int32)
    lived = live != 0
    before = (j[None, :] < j[:, None]) & lived[None, :]

    def prev(key):
        return jnp.max(jnp.where(before & (key[None, :] == key[:, None]), j[None, :], -1), axis=1)

    def last(key):
        hit = lived[None, :] & (key[None, :] == j[:, None])
        return jnp.max(jnp.where(hit, j[None, :], -1), axis=1)

    out = jnp.stack([rows, cols, prev(cols), prev(rows), last(cols), last(rows), rows, cols])
    return jnp.where(out < 0, slots, out)


def shards(green, block_rows, block_cols, block_live, data, row_weight, source_gain):
    slots = green.shape[1]
    src, tm = lax.axis_size("src"), lax.axis_size("tm")
    ny, nx = src // NZ, tm // NC
    cb = source_gain.shape[0] // BS
    rb = src
    per = cb // tm
    datasets = data.shape[2]
    tab = tables(block_rows[0], block_cols[0], block_live[0], slots, rb, cb)
    src_copies = (NZ - 1) + (ny - 1) * NZ
    tm_copies = nx + (nx - 1) + (nx - 1) + nx
    copies = 2 * (2 * src_copies + tm_copies + (NZ - 1) + (ny * nx - 1) + (NC - 1))
    vmem = pl.BlockSpec(memory_space=pltpu.VMEM)
    tile = (BS, BS)
    coded = (BS + 16, BS)
    sol, res, mis = pl.pallas_call(
        functools.partial(kernel, ny, nx, float(src * tm * BS), slots, cb),
        out_shape=(
            jax.ShapeDtypeStruct((per * BS, datasets), F32),
            jax.ShapeDtypeStruct(tile, F32),
            jax.ShapeDtypeStruct((2, datasets), F32),
        ),
        in_specs=[
            pl.BlockSpec(memory_space=pltpu.SMEM),
            pl.BlockSpec(memory_space=pl.ANY),
            vmem, vmem, vmem,
        ],
        out_specs=(vmem, vmem, vmem),
        scratch_shapes=[
            pltpu.VMEM((slots,) + tile, BF16),
            pltpu.VMEM((2, ny, NZ) + tile, BF16),
            pltpu.VMEM((slots + 1,) + tile, F32),
            pltpu.VMEM((2, nx * per) + tile, F32),
            pltpu.VMEM((2, nx * per) + tile, F32),
            pltpu.VMEM((2, nx - 1, per) + coded, jnp.int16),
            pltpu.VMEM((2, nx - 1, per) + coded, jnp.int16),
            pltpu.VMEM((2, cb) + tile, BF16),
            pltpu.VMEM((2, ny - 1, NZ) + coded, jnp.int16),
            pltpu.VMEM((2, ny - 1, NZ) + coded, jnp.int16),
            pltpu.VMEM((2, NZ - 1) + coded, jnp.int16),
            pltpu.VMEM((2, NZ - 1) + coded, jnp.int16),
            pltpu.VMEM(tile, F32),
            pltpu.VMEM((per,) + tile, F32),
            pltpu.VMEM((2, per) + tile, F32),
            pltpu.VMEM((per + 1,) + tile, F32),
            pltpu.VMEM((2, NZ, 8, BS), F32),
            pltpu.VMEM((2, ny * nx, 8, BS), F32),
            pltpu.VMEM((2, NC, 8, BS), F32),
            pltpu.SemaphoreType.DMA((copies,)),
            pltpu.SemaphoreType.DMA((copies,)),
            pltpu.SemaphoreType.DMA,
        ],
        compiler_params=pltpu.CompilerParams(
            collective_id=0, has_side_effects=True, vmem_limit_bytes=48 * 1024 * 1024
        ),
    )(tab, green[0], data[0], row_weight, source_gain.reshape(cb, BS))
    return sol, res[None], mis


def solution(mesh):
    placed = (
        P("tm", "src", None, None),
        P("tm", "src"),
        P("tm", "src"),
        P("tm", "src"),
        P("tm", "src", None),
        P("tm", "src"),
        P("src"),
    )
    return jax.shard_map(
        shards,
        mesh=mesh,
        in_specs=placed,
        out_specs=(P(("src", "tm"), None), P("tm", "src", None), P()),
        check_vma=False,
    )
```

```python
import functools

import jax
import jax.numpy as jnp
from jax import lax
from jax.experimental import pallas as pl
from jax.experimental.pallas import tpu as pltpu
from jax.sharding import PartitionSpec as P

MESH = pl.DeviceIdType.MESH
EPSILON = 1e-06
NZ = 8
NC = 2
BS = 128
F32 = jnp.float32
BF16 = jnp.bfloat16


STEPS = 32000.0


def outward(n):
    return sorted(range(1, n), key=lambda d: -min(d, n - d))


def pack(ref, v):
    top = jnp.maximum(jnp.max(jnp.abs(v), axis=0, keepdims=True), 1e-30)
    e = jnp.ceil(jnp.log2(top))
    q = jnp.floor(v * (jnp.exp2(-e) * STEPS) + 0.5)
    ref[0:BS, :] = q.astype(jnp.int32).astype(jnp.int16)
    ref[BS : BS + 16, :] = jnp.broadcast_to(e.astype(jnp.int32), (16, BS)).astype(jnp.int16)


def unpack(ref):
    e = ref[BS : BS + 16, :].astype(jnp.int32).astype(F32)[0:1]
    return ref[0:BS, :].astype(jnp.int32).astype(F32) * (jnp.exp2(e) * (1.0 / STEPS))


def kernel(
    ny, nx, total_rows, slots, cb,
    tab, green_hbm, data_hbm, weight_hbm, gain_hbm,
    sol_out, res_out, mis_out,
    green, data, weight, gain, ag, wire, acol, sums, core_send, core_recv, x_send, x_recv, tb, y_send, y_recv, z_send, z_recv,
    wcol, gcol, steep, own, ar_z, ar_p, ar_c,
    ssem, rsem, lsem,
):
    nz, nc = NZ, NC
    rb = ny * nz
    per = cb // (nx * nc)
    s = lax.axis_index("src")
    t = lax.axis_index("tm")
    y, z = s // nz, s % nz
    x, c = t // nc, t % nc

    def zdev(d):
        return (y * nz + (z + d) % nz, t)

    def ydev(d):
        return (((y + d) % ny) * nz + z, t)

    def xdev(d):
        return (s, ((x + d) % nx) * nc + c)

    def cdev():
        return (s, x * nc + (1 - c))

    counter = [0]

    def rcopy(src, dst, dev):
        i = counter[0]
        counter[0] += 1
        return pltpu.make_async_remote_copy(
            src_ref=src, dst_ref=dst, send_sem=ssem.at[i], recv_sem=rsem.at[i],
            device_id=dev, device_id_type=MESH,
        )

    pairs = ((weight_hbm, weight), (data_hbm, data), (gain_hbm, gain), (green_hbm, green))
    loads = [pltpu.make_async_copy(a, b, lsem.at[i]) for i, (a, b) in enumerate(pairs)]
    for cp in loads:
        cp.start()

    def pdev(d):
        return (((y + d // nx) % ny) * nz + z, ((x + d % nx) % nx) * nc + c)

    peers = [zdev(d) for d in range(1, nz)] + [pdev(d) for d in range(1, ny * nx)] + [cdev()]
    barrier = pltpu.get_barrier_semaphore()
    for dev in peers:
        pl.semaphore_signal(barrier, inc=1, device_id=dev, device_id_type=MESH)

    for cp in loads[:3]:
        cp.wait()
    wcol[...] = jnp.transpose(jnp.broadcast_to(weight[...], (BS, BS)))
    for i in range(per):
        row = gain[pl.ds(t * per + i, 1), :]
        gcol[i] = jnp.transpose(jnp.broadcast_to(row, (BS, BS)))
    sums[slots] = jnp.zeros((BS, BS), F32)
    res_out[...] = wcol[...] * data[...]
    pl.semaphore_wait(barrier, len(peers))

    def gather_begin(it, v):
        pack(wire.at[it, y, z], jnp.transpose(v))
        mine = wire.at[it, y, z]
        zc = {d: rcopy(mine, mine, zdev(d)) for d in outward(nz)}
        yc = [(rcopy(mine, mine, ydev(e)), e, z) for e in outward(ny)]
        for d in outward(nz):
            zc[d].start()
        for cp, e, zz in yc:
            cp.start()
        return zc, yc

    def gather_relay(it, zc, yc):
        for d in reversed(outward(nz)):
            zc[d].wait_recv()
            zz = (z + nz - d) % nz
            got = wire.at[it, y, zz]
            for e in outward(ny):
                cp = rcopy(got, got, ydev(e))
                cp.start()
                yc.append((cp, e, zz))

    def gather_end(it, zc, yc):
        def use(yy, zz):
            v = unpack(wire.at[0, yy, zz])
            if it:
                v = v - acol[...] * unpack(wire.at[1, yy, zz])
            ag[yy, zz] = v.astype(BF16)

        for zz in range(nz):
            use(y, zz)
        for cp, e, zz in yc:
            cp.wait_recv()
            use((y + ny - e) % ny, zz)
        for cp, e, zz in yc:
            cp.wait_send()
        for d in zc:
            zc[d].wait_send()

    def adjoint():
        def slot(k, carry):
            r = tab[0, k]
            p = jnp.dot(ag[r // nz, r % nz], green[k], preferred_element_type=F32)
            sums[k] = p + sums[tab[2, k]]
            return carry

        lax.fori_loop(0, slots, slot, 0, unroll=16)

    def forward(it):
        def slot(k, carry):
            p = jnp.dot(green[k], tb[it, tab[1, k]], preferred_element_type=F32)
            sums[k] = p + sums[tab[3, k]]
            return carry

        lax.fori_loop(0, slots, slot, 0, unroll=16)

    def scatter_tm(it):
        order = outward(nx) + [0]
        cc = []
        for d in order:
            xx = (x + d) % nx
            for i in range(per):
                b = xx * nc * per + (1 - c) * per + i
                core_send[it, xx * per + i] = sums[tab[4, b]]
            part = pl.ds(xx * per, per)
            cp = rcopy(core_send.at[it, part], core_recv.at[it, part], cdev())
            cp.start()
            cc.append(cp)
        xc = []
        for j, d in enumerate(order):
            xx = (x + d) % nx
            cc[j].wait()
            for i in range(per):
                b = xx * nc * per + c * per + i
                v = sums[tab[4, b]] + core_recv[it, xx * per + i]
                if d:
                    pack(x_send.at[it, d - 1, i], v)
                else:
                    own[i] = v
            if d:
                cp = rcopy(x_send.at[it, d - 1], x_recv.at[it, d - 1], xdev(d))
                cp.start()
                xc.append(cp)
        for cp in xc:
            cp.wait()
        gamma = jnp.zeros((1, BS), F32)
        for i in range(per):
            v = own[i]
            for d in range(1, nx):
                v = v + unpack(x_recv.at[it, d - 1, i])
            st = gcol[i] * jnp.transpose(v)
            steep[it, i] = st
            gamma = gamma + jnp.sum(st * st, axis=0, keepdims=True)
            tb[it, t * per + i] = (gcol[i] * st).astype(BF16)
        return gamma

    def gather_tm(it):
        def part(xx, cc):
            return tb.at[it, pl.ds((xx * nc + cc) * per, per)]

        mine = part(x, c)
        xc = {d: rcopy(mine, mine, xdev(d)) for d in outward(nx)}
        for d in xc:
            xc[d].start()
        fc = [rcopy(mine, mine, cdev())]
        fc[0].start()
        for d in reversed(outward(nx)):
            xc[d].wait_recv()
            got = part((x + nx - d) % nx, c)
            cp = rcopy(got, got, cdev())
            cp.start()
            fc.append(cp)
        for cp in fc:
            cp.wait()
        for d in xc:
            xc[d].wait_send()

    def scatter_src(it):
        order = outward(nz) + [0]
        yc = {}
        for d in order:
            zz = (z + d) % nz
            for e in outward(ny):
                pack(y_send.at[it, e - 1, zz], sums[tab[5, ((y + e) % ny) * nz + zz]])
                yc[d, e] = rcopy(y_send.at[it, e - 1, zz], y_recv.at[it, e - 1, zz], ydev(e))
                yc[d, e].start()
        zc = []
        for d in order:
            zz = (z + d) % nz
            v = sums[tab[5, y * nz + zz]]
            for e in range(1, ny):
                yc[d, e].wait()
                v = v + unpack(y_recv.at[it, e - 1, zz])
            if d:
                pack(z_send.at[it, d - 1], v)
                cp = rcopy(z_send.at[it, d - 1], z_recv.at[it, d - 1], zdev(d))
                cp.start()
                zc.append(cp)
        for cp in zc:
            cp.wait()
        for d in range(1, nz):
            v = v + unpack(z_recv.at[it, d - 1])
        return wcol[...] * v

    stages = ((ar_z, z, nz, zdev), (ar_p, y * nx + x, ny * nx, pdev), (ar_c, c, nc, None))

    def reduce_begin(n, stage, v):
        ref, me, count, dev = stages[stage]
        ref[n, me] = v
        copies = [
            rcopy(ref.at[n, me], ref.at[n, me], dev(d) if dev else cdev())
            for d in range(count - 1, 0, -1)
        ]
        for cp in copies:
            cp.start()
        return copies

    def reduce_end(n, stage, copies):
        ref, me, count, dev = stages[stage]
        for cp in copies:
            cp.wait()
        v = ref[n, 0]
        for j in range(1, count):
            v = v + ref[n, j]
        return v

    def rowsum(a):
        return jnp.sum(a, axis=0, keepdims=True)

    hops = gather_begin(0, wcol[...] * res_out[...])
    gather_relay(0, *hops)
    gather_end(0, *hops)
    loads[3].wait()
    adjoint()
    gamma0 = scatter_tm(0)
    gather_tm(0)
    forward(0)
    image0 = scatter_src(0)
    norms = jnp.concatenate([gamma0, rowsum(image0 * image0), jnp.zeros((6, BS), F32)], axis=0)
    copies = reduce_begin(0, 0, norms)
    own[per] = image0
    hops = gather_begin(1, wcol[...] * image0)
    copies = reduce_begin(0, 1, reduce_end(0, 0, copies))
    gather_relay(1, *hops)
    copies = reduce_begin(0, 2, reduce_end(0, 1, copies))
    norms = reduce_end(0, 2, copies)
    gamma0 = norms[0:1]
    norm0 = norms[1:2]
    alpha0 = gamma0 / (norm0 + EPSILON)
    acol[...] = jnp.transpose(jnp.broadcast_to(alpha0, (BS, BS)))
    gather_end(1, *hops)
    res_out[...] = res_out[...] - alpha0 * own[per]
    adjoint()
    gamma1 = scatter_tm(1)
    gather_tm(1)
    forward(1)
    part1 = scatter_src(1)
    image0 = own[per]
    residual = res_out[...]
    norms = jnp.concatenate(
        [
            gamma1, rowsum(part1 * part1), rowsum(part1 * image0), rowsum(residual * residual),
            rowsum(residual * part1), rowsum(residual * image0), jnp.zeros((2, BS), F32),
        ],
        axis=0,
    )
    for stage in range(3):
        norms = reduce_end(1, stage, reduce_begin(1, stage, norms))
    gamma1 = norms[0:1]
    beta = gamma1 / (gamma0 + EPSILON)
    norm1 = norms[1:2] + beta * (2.0 * norms[2:3] + beta * norm0)
    alpha1 = gamma1 / (norm1 + EPSILON)
    cross = norms[4:5] + beta * norms[5:6]
    misfit1 = norms[3:4] + alpha1 * (alpha1 * norm1 - 2.0 * cross)
    mis_out[0:1, :] = norms[3:4] / total_rows
    mis_out[1:2, :] = misfit1 / total_rows
    res_out[...] = residual - alpha1 * (part1 + beta * image0)
    for i in range(per):
        sol_out[pl.ds(i * BS, BS), :] = (alpha0 + alpha1 * beta) * steep[0, i] + alpha1 * steep[1, i]


def tables(rows, cols, live, slots, rb, cb):
    j = jnp.arange(slots, dtype=jnp.int32)
    lived = live != 0
    before = (j[None, :] < j[:, None]) & lived[None, :]

    def prev(key):
        return jnp.max(jnp.where(before & (key[None, :] == key[:, None]), j[None, :], -1), axis=1)

    def last(key):
        hit = lived[None, :] & (key[None, :] == j[:, None])
        return jnp.max(jnp.where(hit, j[None, :], -1), axis=1)

    out = jnp.stack([rows, cols, prev(cols), prev(rows), last(cols), last(rows), rows, cols])
    return jnp.where(out < 0, slots, out)


def shards(green, block_rows, block_cols, block_live, data, row_weight, source_gain):
    slots = green.shape[1]
    src, tm = lax.axis_size("src"), lax.axis_size("tm")
    ny, nx = src // NZ, tm // NC
    cb = source_gain.shape[0] // BS
    rb = src
    per = cb // tm
    datasets = data.shape[2]
    tab = tables(block_rows[0], block_cols[0], block_live[0], slots, rb, cb)
    src_copies = (NZ - 1) + (ny - 1) * NZ
    tm_copies = nx + (nx - 1) + (nx - 1) + nx
    copies = 2 * (2 * src_copies + tm_copies + (NZ - 1) + (ny * nx - 1) + (NC - 1))
    vmem = pl.BlockSpec(memory_space=pltpu.VMEM)
    hbm = pl.BlockSpec(memory_space=pltpu.HBM)
    tile = (BS, BS)
    coded = (BS + 16, BS)
    sol, res, mis = pl.pallas_call(
        functools.partial(kernel, ny, nx, float(src * tm * BS), slots, cb),
        out_shape=(
            jax.ShapeDtypeStruct((per * BS, datasets), F32),
            jax.ShapeDtypeStruct(tile, F32),
            jax.ShapeDtypeStruct((2, datasets), F32),
        ),
        in_specs=[
            pl.BlockSpec(memory_space=pltpu.SMEM),
            hbm, hbm, hbm, hbm,
        ],
        out_specs=(vmem, vmem, vmem),
        scratch_shapes=[
            pltpu.VMEM((slots,) + tile, BF16),
            pltpu.VMEM(tile, F32),
            pltpu.VMEM((1, BS), F32),
            pltpu.VMEM((cb, BS), F32),
            pltpu.VMEM((ny, NZ) + tile, BF16),
            pltpu.VMEM((2, ny, NZ) + coded, jnp.int16),
            pltpu.VMEM(tile, F32),
            pltpu.VMEM((slots + 1,) + tile, F32),
            pltpu.VMEM((2, nx * per) + tile, F32),
            pltpu.VMEM((2, nx * per) + tile, F32),
            pltpu.VMEM((2, nx - 1, per) + coded, jnp.int16),
            pltpu.VMEM((2, nx - 1, per) + coded, jnp.int16),
            pltpu.VMEM((2, cb) + tile, BF16),
            pltpu.VMEM((2, ny - 1, NZ) + coded, jnp.int16),
            pltpu.VMEM((2, ny - 1, NZ) + coded, jnp.int16),
            pltpu.VMEM((2, NZ - 1) + coded, jnp.int16),
            pltpu.VMEM((2, NZ - 1) + coded, jnp.int16),
            pltpu.VMEM(tile, F32),
            pltpu.VMEM((per,) + tile, F32),
            pltpu.VMEM((2, per) + tile, F32),
            pltpu.VMEM((per + 1,) + tile, F32),
            pltpu.VMEM((2, NZ, 8, BS), F32),
            pltpu.VMEM((2, ny * nx, 8, BS), F32),
            pltpu.VMEM((2, NC, 8, BS), F32),
            pltpu.SemaphoreType.DMA((copies,)),
            pltpu.SemaphoreType.DMA((copies,)),
            pltpu.SemaphoreType.DMA((4,)),
        ],
        compiler_params=pltpu.CompilerParams(
            collective_id=0, has_side_effects=True, vmem_limit_bytes=48 * 1024 * 1024
        ),
    )(tab, green[0], data[0], row_weight, source_gain.reshape(cb, BS))
    return sol, res[None], mis


def solution(mesh):
    placed = (
        P("tm", "src", None, None),
        P("tm", "src"),
        P("tm", "src"),
        P("tm", "src"),
        P("tm", "src", None),
        P("tm", "src"),
        P("src"),
    )
    return jax.shard_map(
        shards,
        mesh=mesh,
        in_specs=placed,
        out_specs=(P(("src", "tm"), None), P("tm", "src", None), P()),
        check_vma=False,
    )
```

```python
import functools

import jax
import jax.numpy as jnp
from jax import lax
from jax.experimental import pallas as pl
from jax.experimental.pallas import tpu as pltpu
from jax.sharding import PartitionSpec as P

MESH = pl.DeviceIdType.MESH
EPSILON = 1e-06
NZ = 8
NC = 2
BS = 128
F32 = jnp.float32
BF16 = jnp.bfloat16


STEPS = 32000.0


def outward(n):
    return sorted(range(1, n), key=lambda d: -min(d, n - d))


def pack(ref, v):
    top = jnp.maximum(jnp.max(jnp.abs(v), axis=0, keepdims=True), 1e-30)
    e = jnp.ceil(jnp.log2(top))
    q = jnp.floor(v * (jnp.exp2(-e) * STEPS) + 0.5)
    ref[0:BS, :] = q.astype(jnp.int32).astype(jnp.int16)
    ref[BS : BS + 16, :] = jnp.broadcast_to(e.astype(jnp.int32), (16, BS)).astype(jnp.int16)


def unpack(ref):
    e = ref[BS : BS + 16, :].astype(jnp.int32).astype(F32)[0:1]
    return ref[0:BS, :].astype(jnp.int32).astype(F32) * (jnp.exp2(e) * (1.0 / STEPS))


def kernel(
    ny, nx, total_rows, slots, cb,
    rows, cols, live, green_hbm, data_hbm, weight_hbm, gain_hbm,
    sol_out, res_out, mis_out,
    tabv, tab, green, data, weight, gain, ag, wire, acol, sums, core_send, core_recv, x_send, x_recv, tb, y_send, y_recv, z_send, z_recv,
    wcol, gcol, steep, own, ar_z, ar_p, ar_c,
    ssem, rsem, lsem,
):
    nz, nc = NZ, NC
    rb = ny * nz
    per = cb // (nx * nc)
    s = lax.axis_index("src")
    t = lax.axis_index("tm")
    y, z = s // nz, s % nz
    x, c = t // nc, t % nc

    def zdev(d):
        return (y * nz + (z + d) % nz, t)

    def ydev(d):
        return (((y + d) % ny) * nz + z, t)

    def xdev(d):
        return (s, ((x + d) % nx) * nc + c)

    def cdev():
        return (s, x * nc + (1 - c))

    counter = [0]

    def rcopy(src, dst, dev):
        i = counter[0]
        counter[0] += 1
        return pltpu.make_async_remote_copy(
            src_ref=src, dst_ref=dst, send_sem=ssem.at[i], recv_sem=rsem.at[i],
            device_id=dev, device_id_type=MESH,
        )

    pairs = ((weight_hbm, weight), (data_hbm, data), (gain_hbm, gain), (green_hbm, green))
    loads = [pltpu.make_async_copy(a, b, lsem.at[i]) for i, (a, b) in enumerate(pairs)]
    for cp in loads:
        cp.start()

    def pdev(d):
        return (((y + d // nx) % ny) * nz + z, ((x + d % nx) % nx) * nc + c)

    peers = [zdev(d) for d in range(1, nz)] + [pdev(d) for d in range(1, ny * nx)] + [cdev()]
    barrier = pltpu.get_barrier_semaphore()
    for dev in peers:
        pl.semaphore_signal(barrier, inc=1, device_id=dev, device_id_type=MESH)

    for cp in loads[:3]:
        cp.wait()
    tabv[...] = jnp.zeros((8, slots), jnp.int32)
    wcol[...] = jnp.transpose(jnp.broadcast_to(weight[...], (BS, BS)))
    for i in range(per):
        row = gain[pl.ds(t * per + i, 1), :]
        gcol[i] = jnp.transpose(jnp.broadcast_to(row, (BS, BS)))
    sums[slots] = jnp.zeros((BS, BS), F32)
    res_out[...] = wcol[...] * data[...]
    pl.semaphore_wait(barrier, len(peers))

    def gather_begin(it, v):
        pack(wire.at[it, y, z], jnp.transpose(v))
        mine = wire.at[it, y, z]
        zc = {d: rcopy(mine, mine, zdev(d)) for d in outward(nz)}
        yc = [(rcopy(mine, mine, ydev(e)), e, z) for e in outward(ny)]
        for d in reversed(outward(nz)):
            zc[d].start()
        for cp, e, zz in yc:
            cp.start()
        return zc, yc

    def gather_relay(it, zc, yc):
        for d in reversed(outward(nz)):
            zc[d].wait_recv()
            zz = (z + nz - d) % nz
            got = wire.at[it, y, zz]
            for e in outward(ny):
                cp = rcopy(got, got, ydev(e))
                cp.start()
                yc.append((cp, e, zz))

    def gather_end(it, zc, yc):
        def use(yy, zz):
            v = unpack(wire.at[0, yy, zz])
            if it:
                v = v - acol[...] * unpack(wire.at[1, yy, zz])
            ag[yy, zz] = v.astype(BF16)

        for zz in range(nz):
            use(y, zz)
        for cp, e, zz in yc:
            cp.wait_recv()
            use((y + ny - e) % ny, zz)
        for cp, e, zz in yc:
            cp.wait_send()
        for d in zc:
            zc[d].wait_send()

    def tables():
        jj = lax.broadcasted_iota(jnp.int32, (slots, slots), 0)
        kk = lax.broadcasted_iota(jnp.int32, (slots, slots), 1)

        def latest(hit):
            j = jnp.max(jnp.where(hit, jj, -1), axis=0, keepdims=True)
            return jnp.where(j < 0, slots, j)

        tabv[0:1, :] = rows[...]
        tabv[1:2, :] = cols[...]
        for n, key in enumerate((cols, rows)):
            lived = jnp.where(live[...] != 0, key[...], -1)
            down = jnp.transpose(jnp.broadcast_to(lived, (slots, slots)))
            tabv[2 + n : 3 + n, :] = latest((down == key[...]) & (jj < kk))
            tabv[4 + n : 5 + n, :] = latest(down == kk)
        cp = pltpu.make_async_copy(tabv, tab, lsem.at[4])
        cp.start()
        cp.wait()

    def adjoint():
        def slot(k, carry):
            r = tab[0, k]
            p = jnp.dot(ag[r // nz, r % nz], green[k], preferred_element_type=F32)
            sums[k] = p + sums[tab[2, k]]
            return carry

        lax.fori_loop(0, slots, slot, 0, unroll=32)

    def forward(it):
        def slot(k, carry):
            p = jnp.dot(green[k], tb[it, tab[1, k]], preferred_element_type=F32)
            sums[k] = p + sums[tab[3, k]]
            return carry

        lax.fori_loop(0, slots, slot, 0, unroll=32)

    def exchange_tm(it):
        cc = []
        for i in range(per):
            for d in outward(nx) + [0]:
                xx = (x + d) % nx
                core_send[it, i, xx] = sums[tab[4, (xx * nc + 1 - c) * per + i]]
            cp = rcopy(core_send.at[it, i], core_recv.at[it, i], cdev())
            cp.start()
            cc.append(cp)
        xc = {}
        for i in range(per):
            cc[i].wait()
            for d in outward(nx) + [0]:
                xx = (x + d) % nx
                v = sums[tab[4, (xx * nc + c) * per + i]] + core_recv[it, i, xx]
                if d:
                    pack(x_send.at[it, d - 1, i], v)
                    xc[i, d] = rcopy(x_send.at[it, d - 1, i], x_recv.at[it, d - 1, i], xdev(d))
                    xc[i, d].start()
                else:
                    own[i] = v
        gamma = jnp.zeros((1, BS), F32)
        gc, fc = {}, []
        for i in range(per):
            v = own[i]
            for d in range(1, nx):
                xc[i, d].wait()
                v = v + unpack(x_recv.at[it, d - 1, i])
            st = gcol[i] * jnp.transpose(v)
            steep[it, i] = st
            gamma = gamma + jnp.sum(st * st, axis=0, keepdims=True)
            mine = tb.at[it, t * per + i]
            tb[it, t * per + i] = (gcol[i] * st).astype(BF16)
            for d in outward(nx):
                gc[i, d] = rcopy(mine, mine, xdev(d))
                gc[i, d].start()
            fc.append(rcopy(mine, mine, cdev()))
            fc[-1].start()
        for i in range(per):
            for d in reversed(outward(nx)):
                gc[i, d].wait_recv()
                got = tb.at[it, (((x + nx - d) % nx) * nc + c) * per + i]
                fc.append(rcopy(got, got, cdev()))
                fc[-1].start()
        for cp in fc:
            cp.wait()
        for key in gc:
            gc[key].wait_send()
        return gamma

    def scatter_src(it):
        order = outward(nz) + [0]
        yc = {}
        for d in order:
            zz = (z + d) % nz
            for e in outward(ny):
                pack(y_send.at[it, e - 1, zz], sums[tab[5, ((y + e) % ny) * nz + zz]])
                yc[d, e] = rcopy(y_send.at[it, e - 1, zz], y_recv.at[it, e - 1, zz], ydev(e))
                yc[d, e].start()
        zc = []
        for d in order:
            zz = (z + d) % nz
            v = sums[tab[5, y * nz + zz]]
            for e in range(1, ny):
                yc[d, e].wait()
                v = v + unpack(y_recv.at[it, e - 1, zz])
            if d:
                pack(z_send.at[it, d - 1], v)
                cp = rcopy(z_send.at[it, d - 1], z_recv.at[it, d - 1], zdev(d))
                cp.start()
                zc.append(cp)
        for cp in zc:
            cp.wait()
        for d in range(1, nz):
            v = v + unpack(z_recv.at[it, d - 1])
        return wcol[...] * v

    stages = ((ar_z, z, nz, zdev), (ar_p, y * nx + x, ny * nx, pdev), (ar_c, c, nc, None))

    def reduce_begin(n, stage, v):
        ref, me, count, dev = stages[stage]
        ref[n, me] = v
        copies = [
            rcopy(ref.at[n, me], ref.at[n, me], dev(d) if dev else cdev())
            for d in range(count - 1, 0, -1)
        ]
        for cp in copies:
            cp.start()
        return copies

    def reduce_end(n, stage, copies):
        ref, me, count, dev = stages[stage]
        for cp in copies:
            cp.wait()
        v = ref[n, 0]
        for j in range(1, count):
            v = v + ref[n, j]
        return v

    def rowsum(a):
        return jnp.sum(a, axis=0, keepdims=True)

    hops = gather_begin(0, wcol[...] * res_out[...])
    tables()
    gather_relay(0, *hops)
    gather_end(0, *hops)
    loads[3].wait()
    adjoint()
    gamma0 = exchange_tm(0)
    forward(0)
    image0 = scatter_src(0)
    norms = jnp.concatenate([gamma0, rowsum(image0 * image0), jnp.zeros((6, BS), F32)], axis=0)
    copies = reduce_begin(0, 0, norms)
    own[per] = image0
    hops = gather_begin(1, wcol[...] * image0)
    copies = reduce_begin(0, 1, reduce_end(0, 0, copies))
    gather_relay(1, *hops)
    copies = reduce_begin(0, 2, reduce_end(0, 1, copies))
    norms = reduce_end(0, 2, copies)
    gamma0 = norms[0:1]
    norm0 = norms[1:2]
    alpha0 = gamma0 / (norm0 + EPSILON)
    acol[...] = jnp.transpose(jnp.broadcast_to(alpha0, (BS, BS)))
    gather_end(1, *hops)
    res_out[...] = res_out[...] - alpha0 * own[per]
    adjoint()
    gamma1 = exchange_tm(1)
    forward(1)
    part1 = scatter_src(1)
    image0 = own[per]
    residual = res_out[...]
    norms = jnp.concatenate(
        [
            gamma1, rowsum(part1 * part1), rowsum(part1 * image0), rowsum(residual * residual),
            rowsum(residual * part1), rowsum(residual * image0), jnp.zeros((2, BS), F32),
        ],
        axis=0,
    )
    for stage in range(3):
        norms = reduce_end(1, stage, reduce_begin(1, stage, norms))
    gamma1 = norms[0:1]
    beta = gamma1 / (gamma0 + EPSILON)
    norm1 = norms[1:2] + beta * (2.0 * norms[2:3] + beta * norm0)
    alpha1 = gamma1 / (norm1 + EPSILON)
    cross = norms[4:5] + beta * norms[5:6]
    misfit1 = norms[3:4] + alpha1 * (alpha1 * norm1 - 2.0 * cross)
    mis_out[0:1, :] = norms[3:4] / total_rows
    mis_out[1:2, :] = misfit1 / total_rows
    res_out[...] = residual - alpha1 * (part1 + beta * image0)
    for i in range(per):
        sol_out[pl.ds(i * BS, BS), :] = (alpha0 + alpha1 * beta) * steep[0, i] + alpha1 * steep[1, i]


def shards(green, block_rows, block_cols, block_live, data, row_weight, source_gain):
    slots = green.shape[1]
    src, tm = lax.axis_size("src"), lax.axis_size("tm")
    ny, nx = src // NZ, tm // NC
    cb = source_gain.shape[0] // BS
    per = cb // tm
    datasets = data.shape[2]
    src_copies = (NZ - 1) + (ny - 1) * NZ
    tm_copies = per * (1 + (nx - 1) + (nx - 1) + nx)
    copies = 2 * (2 * src_copies + tm_copies + (NZ - 1) + (ny * nx - 1) + (NC - 1))
    vmem = pl.BlockSpec(memory_space=pltpu.VMEM)
    hbm = pl.BlockSpec(memory_space=pltpu.HBM)
    tile = (BS, BS)
    coded = (BS + 16, BS)
    sol, res, mis = pl.pallas_call(
        functools.partial(kernel, ny, nx, float(src * tm * BS), slots, cb),
        out_shape=(
            jax.ShapeDtypeStruct((per * BS, datasets), F32),
            jax.ShapeDtypeStruct(tile, F32),
            jax.ShapeDtypeStruct((2, datasets), F32),
        ),
        in_specs=[
            vmem, vmem, vmem, hbm, hbm, hbm, hbm,
        ],
        out_specs=(vmem, vmem, vmem),
        scratch_shapes=[
            pltpu.VMEM((8, slots), jnp.int32),
            pltpu.SMEM((8, slots), jnp.int32),
            pltpu.VMEM((slots,) + tile, BF16),
            pltpu.VMEM(tile, F32),
            pltpu.VMEM((1, BS), F32),
            pltpu.VMEM((cb, BS), F32),
            pltpu.VMEM((ny, NZ) + tile, BF16),
            pltpu.VMEM((2, ny, NZ) + coded, jnp.int16),
            pltpu.VMEM(tile, F32),
            pltpu.VMEM((slots + 1,) + tile, F32),
            pltpu.VMEM((2, per, nx) + tile, F32),
            pltpu.VMEM((2, per, nx) + tile, F32),
            pltpu.VMEM((2, nx - 1, per) + coded, jnp.int16),
            pltpu.VMEM((2, nx - 1, per) + coded, jnp.int16),
            pltpu.VMEM((2, cb) + tile, BF16),
            pltpu.VMEM((2, ny - 1, NZ) + coded, jnp.int16),
            pltpu.VMEM((2, ny - 1, NZ) + coded, jnp.int16),
            pltpu.VMEM((2, NZ - 1) + coded, jnp.int16),
            pltpu.VMEM((2, NZ - 1) + coded, jnp.int16),
            pltpu.VMEM(tile, F32),
            pltpu.VMEM((per,) + tile, F32),
            pltpu.VMEM((2, per) + tile, F32),
            pltpu.VMEM((per + 1,) + tile, F32),
            pltpu.VMEM((2, NZ, 8, BS), F32),
            pltpu.VMEM((2, ny * nx, 8, BS), F32),
            pltpu.VMEM((2, NC, 8, BS), F32),
            pltpu.SemaphoreType.DMA((copies,)),
            pltpu.SemaphoreType.DMA((copies,)),
            pltpu.SemaphoreType.DMA((5,)),
        ],
        compiler_params=pltpu.CompilerParams(
            collective_id=0, has_side_effects=True, vmem_limit_bytes=48 * 1024 * 1024
        ),
    )(block_rows, block_cols, block_live, green[0], data[0], row_weight, source_gain.reshape(cb, BS))
    return sol, res[None], mis


def solution(mesh):
    placed = (
        P("tm", "src", None, None),
        P("tm", "src"),
        P("tm", "src"),
        P("tm", "src"),
        P("tm", "src", None),
        P("tm", "src"),
        P("src"),
    )
    return jax.shard_map(
        shards,
        mesh=mesh,
        in_specs=placed,
        out_specs=(P(("src", "tm"), None), P("tm", "src", None), P()),
        check_vma=False,
    )
```

```python
import functools

import jax
import jax.numpy as jnp
from jax import lax
from jax.experimental import pallas as pl
from jax.experimental.pallas import tpu as pltpu
from jax.sharding import PartitionSpec as P

MESH = pl.DeviceIdType.MESH
EPSILON = 1e-06
NZ = 8
NC = 2
BS = 128
F32 = jnp.float32
BF16 = jnp.bfloat16


STEPS = 32000.0


def outward(n):
    return sorted(range(1, n), key=lambda d: -min(d, n - d))


def pack(ref, v):
    top = jnp.maximum(jnp.max(jnp.abs(v), axis=0, keepdims=True), 1e-30)
    e = jnp.ceil(jnp.log2(top))
    q = jnp.floor(v * (jnp.exp2(-e) * STEPS) + 0.5)
    ref[0:BS, :] = q.astype(jnp.int32).astype(jnp.int16)
    ref[BS : BS + 8, :] = jnp.broadcast_to(e.astype(jnp.int32), (8, BS)).astype(jnp.int16)


def unpack(ref):
    e = ref[BS : BS + 8, :].astype(jnp.int32).astype(F32)[0:1]
    return ref[0:BS, :].astype(jnp.int32).astype(F32) * (jnp.exp2(e) * (1.0 / STEPS))


def kernel(
    ny, nx, total_rows, slots, cb,
    rows, cols, live, green_hbm, data_hbm, weight_hbm, gain_hbm,
    sol_out, res_out, mis_out,
    tabv, tab, green, data, weight, gain, ag, wire, acol, sums, core_send, core_recv, x_send, x_recv, tb, y_send, y_recv, z_send, z_recv,
    wcol, gcol, steep, own, ar_z, ar_p, ar_c,
    ssem, rsem, lsem,
):
    nz, nc = NZ, NC
    rb = ny * nz
    per = cb // (nx * nc)
    s = lax.axis_index("src")
    t = lax.axis_index("tm")
    y, z = s // nz, s % nz
    x, c = t // nc, t % nc

    def zdev(d):
        return (y * nz + (z + d) % nz, t)

    def ydev(d):
        return (((y + d) % ny) * nz + z, t)

    def xdev(d):
        return (s, ((x + d) % nx) * nc + c)

    def cdev():
        return (s, x * nc + (1 - c))

    counter = [0]

    def rcopy(src, dst, dev):
        i = counter[0]
        counter[0] += 1
        return pltpu.make_async_remote_copy(
            src_ref=src, dst_ref=dst, send_sem=ssem.at[i], recv_sem=rsem.at[i],
            device_id=dev, device_id_type=MESH,
        )

    pairs = ((weight_hbm, weight), (data_hbm, data), (gain_hbm, gain), (green_hbm, green))
    loads = [pltpu.make_async_copy(a, b, lsem.at[i]) for i, (a, b) in enumerate(pairs)]
    for cp in loads:
        cp.start()

    def pdev(d):
        return (((y + d // nx) % ny) * nz + z, ((x + d % nx) % nx) * nc + c)

    peers = [zdev(d) for d in range(1, nz)] + [pdev(d) for d in range(1, ny * nx)] + [cdev()]
    barrier = pltpu.get_barrier_semaphore()
    for dev in peers:
        pl.semaphore_signal(barrier, inc=1, device_id=dev, device_id_type=MESH)

    for cp in loads[:3]:
        cp.wait()
    tabv[...] = jnp.zeros((8, slots), jnp.int32)
    wcol[...] = jnp.transpose(jnp.broadcast_to(weight[...], (BS, BS)))
    for i in range(per):
        row = gain[pl.ds(t * per + i, 1), :]
        gcol[i] = jnp.transpose(jnp.broadcast_to(row, (BS, BS)))
    sums[slots] = jnp.zeros((BS, BS), F32)
    res_out[...] = wcol[...] * data[...]
    pack(wire.at[0, y, z], jnp.transpose(wcol[...] * res_out[...]))
    pl.semaphore_wait(barrier, len(peers))

    def gather_begin(it):
        mine = wire.at[it, y, z]
        zc = {d: rcopy(mine, mine, zdev(d)) for d in outward(nz)}
        yc = [(rcopy(mine, mine, ydev(e)), e, z) for e in outward(ny)]
        for d in reversed(outward(nz)):
            zc[d].start()
        for cp, e, zz in yc:
            cp.start()
        return zc, yc

    def gather_relay(it, zc, yc):
        for d in reversed(outward(nz)):
            zc[d].wait_recv()
            zz = (z + nz - d) % nz
            got = wire.at[it, y, zz]
            for e in outward(ny):
                cp = rcopy(got, got, ydev(e))
                cp.start()
                yc.append((cp, e, zz))

    def gather_end(it, zc, yc):
        def use(yy, zz):
            v = unpack(wire.at[0, yy, zz])
            if it:
                v = v - acol[...] * unpack(wire.at[1, yy, zz])
            ag[yy, zz] = v.astype(BF16)

        for zz in range(nz):
            use(y, zz)
        for cp, e, zz in yc:
            cp.wait_recv()
            use((y + ny - e) % ny, zz)
        for cp, e, zz in yc:
            cp.wait_send()
        for d in zc:
            zc[d].wait_send()

    def tables():
        jj = lax.broadcasted_iota(jnp.int32, (slots, slots), 0)
        kk = lax.broadcasted_iota(jnp.int32, (slots, slots), 1)

        def latest(hit):
            j = jnp.max(jnp.where(hit, jj, -1), axis=0, keepdims=True)
            return jnp.where(j < 0, slots, j)

        tabv[0:1, :] = rows[...]
        tabv[1:2, :] = cols[...]
        for n, key in enumerate((cols, rows)):
            lived = jnp.where(live[...] != 0, key[...], -1)
            down = jnp.transpose(jnp.broadcast_to(lived, (slots, slots)))
            tabv[2 + n : 3 + n, :] = latest((down == key[...]) & (jj < kk))
            tabv[4 + n : 5 + n, :] = latest(down == kk)
        cp = pltpu.make_async_copy(tabv, tab, lsem.at[4])
        cp.start()
        cp.wait()

    def adjoint():
        def slot(k, carry):
            r = tab[0, k]
            p = jnp.dot(ag[r // nz, r % nz], green[k], preferred_element_type=F32)
            sums[k] = p + sums[tab[2, k]]
            return carry

        lax.fori_loop(0, slots, slot, 0, unroll=32)

    def forward(it):
        def slot(k, carry):
            p = jnp.dot(green[k], tb[it, tab[1, k]], preferred_element_type=F32)
            sums[k] = p + sums[tab[3, k]]
            return carry

        lax.fori_loop(0, slots, slot, 0, unroll=32)

    def exchange_tm(it):
        cc = []
        for i in range(per):
            for d in outward(nx) + [0]:
                xx = (x + d) % nx
                core_send[it, i, xx] = sums[tab[4, (xx * nc + 1 - c) * per + i]]
            cp = rcopy(core_send.at[it, i], core_recv.at[it, i], cdev())
            cp.start()
            cc.append(cp)
        xc = {}
        for i in range(per):
            cc[i].wait()
            for d in outward(nx) + [0]:
                xx = (x + d) % nx
                v = sums[tab[4, (xx * nc + c) * per + i]] + core_recv[it, i, xx]
                if d:
                    pack(x_send.at[it, d - 1, i], v)
                    xc[i, d] = rcopy(x_send.at[it, d - 1, i], x_recv.at[it, d - 1, i], xdev(d))
                    xc[i, d].start()
                else:
                    own[i] = v
        gamma = jnp.zeros((1, BS), F32)
        gc, fc = {}, []
        for i in range(per):
            v = own[i]
            for d in range(1, nx):
                xc[i, d].wait()
                v = v + unpack(x_recv.at[it, d - 1, i])
            st = gcol[i] * jnp.transpose(v)
            steep[it, i] = st
            gamma = gamma + jnp.sum(st * st, axis=0, keepdims=True)
            mine = tb.at[it, t * per + i]
            tb[it, t * per + i] = (gcol[i] * st).astype(BF16)
            for d in outward(nx):
                gc[i, d] = rcopy(mine, mine, xdev(d))
                gc[i, d].start()
            fc.append(rcopy(mine, mine, cdev()))
            fc[-1].start()
        for i in range(per):
            for d in reversed(outward(nx)):
                gc[i, d].wait_recv()
                got = tb.at[it, (((x + nx - d) % nx) * nc + c) * per + i]
                fc.append(rcopy(got, got, cdev()))
                fc[-1].start()
        for cp in fc:
            cp.wait()
        for key in gc:
            gc[key].wait_send()
        return gamma

    def scatter_src(it):
        order = outward(nz) + [0]
        yc = {}
        for d in order:
            zz = (z + d) % nz
            for e in outward(ny):
                pack(y_send.at[it, e - 1, zz], sums[tab[5, ((y + e) % ny) * nz + zz]])
                yc[d, e] = rcopy(y_send.at[it, e - 1, zz], y_recv.at[it, e - 1, zz], ydev(e))
                yc[d, e].start()
        zc = []
        for d in order:
            zz = (z + d) % nz
            v = sums[tab[5, y * nz + zz]]
            for e in range(1, ny):
                yc[d, e].wait()
                v = v + unpack(y_recv.at[it, e - 1, zz])
            if d:
                pack(z_send.at[it, d - 1], v)
                cp = rcopy(z_send.at[it, d - 1], z_recv.at[it, d - 1], zdev(d))
                cp.start()
                zc.append(cp)
        for cp in zc:
            cp.wait()
        for d in range(1, nz):
            v = v + unpack(z_recv.at[it, d - 1])
        return wcol[...] * v

    stages = ((ar_z, z, nz, zdev), (ar_p, y * nx + x, ny * nx, pdev), (ar_c, c, nc, None))

    def reduce_begin(n, stage, v):
        ref, me, count, dev = stages[stage]
        ref[n, me] = v
        copies = [
            rcopy(ref.at[n, me], ref.at[n, me], dev(d) if dev else cdev())
            for d in range(count - 1, 0, -1)
        ]
        for cp in copies:
            cp.start()
        return copies

    def reduce_end(n, stage, copies):
        ref, me, count, dev = stages[stage]
        for cp in copies:
            cp.wait()
        v = ref[n, 0]
        for j in range(1, count):
            v = v + ref[n, j]
        return v

    def rowsum(a):
        return jnp.sum(a, axis=0, keepdims=True)

    hops = gather_begin(0)
    tables()
    gather_relay(0, *hops)
    gather_end(0, *hops)
    loads[3].wait()
    adjoint()
    gamma0 = exchange_tm(0)
    forward(0)
    image0 = scatter_src(0)
    norms = jnp.concatenate([gamma0, rowsum(image0 * image0), jnp.zeros((6, BS), F32)], axis=0)
    copies = reduce_begin(0, 0, norms)
    own[per] = image0
    pack(wire.at[1, y, z], jnp.transpose(wcol[...] * image0))
    hops = gather_begin(1)
    copies = reduce_begin(0, 1, reduce_end(0, 0, copies))
    gather_relay(1, *hops)
    copies = reduce_begin(0, 2, reduce_end(0, 1, copies))
    norms = reduce_end(0, 2, copies)
    gamma0 = norms[0:1]
    norm0 = norms[1:2]
    alpha0 = gamma0 / (norm0 + EPSILON)
    acol[...] = jnp.transpose(jnp.broadcast_to(alpha0, (BS, BS)))
    gather_end(1, *hops)
    res_out[...] = res_out[...] - alpha0 * own[per]
    adjoint()
    gamma1 = exchange_tm(1)
    forward(1)
    part1 = scatter_src(1)
    image0 = own[per]
    residual = res_out[...]
    norms = jnp.concatenate(
        [
            gamma1, rowsum(part1 * part1), rowsum(part1 * image0), rowsum(residual * residual),
            rowsum(residual * part1), rowsum(residual * image0), jnp.zeros((2, BS), F32),
        ],
        axis=0,
    )
    for stage in range(3):
        norms = reduce_end(1, stage, reduce_begin(1, stage, norms))
    gamma1 = norms[0:1]
    beta = gamma1 / (gamma0 + EPSILON)
    norm1 = norms[1:2] + beta * (2.0 * norms[2:3] + beta * norm0)
    alpha1 = gamma1 / (norm1 + EPSILON)
    cross = norms[4:5] + beta * norms[5:6]
    misfit1 = norms[3:4] + alpha1 * (alpha1 * norm1 - 2.0 * cross)
    mis_out[0:1, :] = norms[3:4] / total_rows
    mis_out[1:2, :] = misfit1 / total_rows
    res_out[...] = residual - alpha1 * (part1 + beta * image0)
    for i in range(per):
        sol_out[pl.ds(i * BS, BS), :] = (alpha0 + alpha1 * beta) * steep[0, i] + alpha1 * steep[1, i]


def shards(green, block_rows, block_cols, block_live, data, row_weight, source_gain):
    slots = green.shape[1]
    src, tm = lax.axis_size("src"), lax.axis_size("tm")
    ny, nx = src // NZ, tm // NC
    cb = source_gain.shape[0] // BS
    per = cb // tm
    datasets = data.shape[2]
    src_copies = (NZ - 1) + (ny - 1) * NZ
    tm_copies = per * (1 + (nx - 1) + (nx - 1) + nx)
    copies = 2 * (2 * src_copies + tm_copies + (NZ - 1) + (ny * nx - 1) + (NC - 1))
    vmem = pl.BlockSpec(memory_space=pltpu.VMEM)
    hbm = pl.BlockSpec(memory_space=pltpu.HBM)
    tile = (BS, BS)
    coded = (BS + 8, BS)
    sol, res, mis = pl.pallas_call(
        functools.partial(kernel, ny, nx, float(src * tm * BS), slots, cb),
        out_shape=(
            jax.ShapeDtypeStruct((per * BS, datasets), F32),
            jax.ShapeDtypeStruct(tile, F32),
            jax.ShapeDtypeStruct((2, datasets), F32),
        ),
        in_specs=[
            vmem, vmem, vmem, hbm, hbm, hbm, hbm,
        ],
        out_specs=(vmem, vmem, vmem),
        scratch_shapes=[
            pltpu.VMEM((8, slots), jnp.int32),
            pltpu.SMEM((8, slots), jnp.int32),
            pltpu.VMEM((slots,) + tile, BF16),
            pltpu.VMEM(tile, F32),
            pltpu.VMEM((1, BS), F32),
            pltpu.VMEM((cb, BS), F32),
            pltpu.VMEM((ny, NZ) + tile, BF16),
            pltpu.VMEM((3, ny, NZ) + coded, jnp.int16),
            pltpu.VMEM(tile, F32),
            pltpu.VMEM((slots + 1,) + tile, F32),
            pltpu.VMEM((2, per, nx) + tile, F32),
            pltpu.VMEM((2, per, nx) + tile, F32),
            pltpu.VMEM((3, nx - 1, per) + coded, jnp.int16),
            pltpu.VMEM((3, nx - 1, per) + coded, jnp.int16),
            pltpu.VMEM((2, cb) + tile, BF16),
            pltpu.VMEM((3, ny - 1, NZ) + coded, jnp.int16),
            pltpu.VMEM((3, ny - 1, NZ) + coded, jnp.int16),
            pltpu.VMEM((3, NZ - 1) + coded, jnp.int16),
            pltpu.VMEM((3, NZ - 1) + coded, jnp.int16),
            pltpu.VMEM(tile, F32),
            pltpu.VMEM((per,) + tile, F32),
            pltpu.VMEM((2, per) + tile, F32),
            pltpu.VMEM((per + 1,) + tile, F32),
            pltpu.VMEM((2, NZ, 8, BS), F32),
            pltpu.VMEM((2, ny * nx, 8, BS), F32),
            pltpu.VMEM((2, NC, 8, BS), F32),
            pltpu.SemaphoreType.DMA((copies,)),
            pltpu.SemaphoreType.DMA((copies,)),
            pltpu.SemaphoreType.DMA((5,)),
        ],
        compiler_params=pltpu.CompilerParams(
            collective_id=0, has_side_effects=True, vmem_limit_bytes=48 * 1024 * 1024
        ),
    )(block_rows, block_cols, block_live, green[0], data[0], row_weight, source_gain.reshape(cb, BS))
    return sol, res[None], mis


def solution(mesh):
    placed = (
        P("tm", "src", None, None),
        P("tm", "src"),
        P("tm", "src"),
        P("tm", "src"),
        P("tm", "src", None),
        P("tm", "src"),
        P("src"),
    )
    return jax.shard_map(
        shards,
        mesh=mesh,
        in_specs=placed,
        out_specs=(P(("src", "tm"), None), P("tm", "src", None), P()),
        check_vma=False,
    )
```
